32 devices in a mesh: seq: 8 (over z, x), dp: 4 (over y, core).
Axes of the slice: x: 2, y: 2, z: 4, core: 2. Of those that a mesh axis runs over, the one named last changes fastest.
Arguments:
- conv_input: bfloat16 [4, 2048, 2816], P('dp', 'seq'), may hold values from -6 to 6
- gate_input: bfloat16 [4, 2048, 2560], P('dp', 'seq'), may hold values from -6 to 6
- step_input: float32 [4, 40, 2048], P('dp', None, 'seq'), may hold values from -7.5 to 2048
- filter_taps: float32 [4, 2816], replicated, may hold values from -3 to 3
- filter_bias: float32 [2816], replicated, may hold values from -0.5 to 0.5
- step_bias: float32 [40], replicated, may hold values from -1 to 1
- decay_log: float32 [40], replicated, may hold values from -13 to 3
- skip_gain: float32 [40], replicated, may hold values from 0.5 to 1.5
- norm_weight: float32 [2560], replicated, may hold values from 0.5 to 1.5
- output_weight: bfloat16 [2560, 1280], P('dp'), may hold values from -0.125 to 0.125
- output_grad: bfloat16 [4, 2048, 1280], P('dp', 'seq'), may hold values from -6 to 6
Outputs:
- input_grad: bfloat16 [4, 2048, 2816], P('dp', 'seq')
- gate_grad: bfloat16 [4, 2048, 2560], P('dp', 'seq')
- step_grad: float32 [4, 40, 2048], P('dp', None, 'seq')
- weight_grad: float32 [2560, 1280], P('dp')
- filter_grads: float32 [5, 2816], replicated
- norm_grad: float32 [2560], replicated
- head_grads: float32 [3, 40], replicated
The draws below stay inside these ranges and needn't reach their ends.
All inputs are finite; a program needn't handle non-finite values.
Results may differ from the reference program's by a relative error of at most 0.0029.
Values may be sent and summed in bfloat16 or wider, within the bound.
A program may use at most 192 MiB of HBM per device.

```python
import jax
import jax.numpy as jnp
from jax import lax

HEADS = 40
HEAD_DIM = 64
STATE = 128
WIDTH = 1280
SPAN = 256
KERNEL = 4
TOKENS_DEV = 256
INNER = 2560
CHANNELS = 2816
SEQ_LEN = 2048
BATCH = 4


def head_rates(key):
    folded = jax.random.fold_in(key, 4099)
    slow_key, fast_key, pick_key = jax.random.split(folded, 3)
    slow_rate = jax.random.uniform(slow_key, (HEADS,), jnp.float32, 10.0, 30.0) / (0.03 * SEQ_LEN)
    fast_rate = 1.0 / (0.03 * jax.random.uniform(fast_key, (HEADS,), jnp.float32, 30.0, 50.0))
    share = 0.5
    chosen = jax.random.uniform(pick_key, (HEADS,), jnp.float32) < share
    return jnp.where(chosen, fast_rate, slow_rate)


def draw_decay_log(key, part):
    return jnp.log(head_rates(key))


def draw_step_input(key, part):
    rates = head_rates(key)
    folded = jax.random.fold_in(key, 8191)
    noise_key, block_key, place_key, loss_key = jax.random.split(folded, 4)
    noise = jax.random.uniform(noise_key, (BATCH, HEADS, SEQ_LEN), jnp.float32, -5.5, -2.5)
    levels = jax.random.uniform(block_key, (BATCH, HEADS, SEQ_LEN // TOKENS_DEV, 1), jnp.float32, -1.0, 1.0)
    spread = jnp.broadcast_to(levels, (BATCH, HEADS, SEQ_LEN // TOKENS_DEV, TOKENS_DEV)).reshape(BATCH, HEADS, SEQ_LEN)
    places = jax.random.randint(place_key, (BATCH, 2), 0, SEQ_LEN)
    marked = jnp.any(jnp.arange(SEQ_LEN)[None, None, :] == places[:, :, None], axis=1)
    losses = jax.random.uniform(loss_key, (BATCH, HEADS, 1), jnp.float32, 0.2, 0.45)
    jumps = -jnp.log(1.0 - losses) / rates[None, :, None]
    return jnp.where(marked[:, None, :], jumps, noise + spread)


def block_levels(rng, extent, cuts, least, high):
    loudness = 1.0
    for dim, parts in cuts:
        draws = jax.random.uniform(jax.random.fold_in(jax.random.fold_in(rng, 6), dim), (parts,), jnp.float32, least / len(cuts), high / len(cuts))
        loudness = loudness * jnp.repeat(jnp.exp(draws), extent[dim] // parts).reshape((-1,) + (1,) * (len(extent) - 1 - dim))
    return loudness


def scatter_about(stream_key, shape, scale, limit, cuts=(), kind=jnp.bfloat16):
    loudness = block_levels(stream_key, shape, cuts, -0.22, 0.18) if cuts else 1.0
    values = jax.random.normal(stream_key, shape, jnp.float32) * scale * loudness
    return jnp.minimum(jnp.maximum(values, -limit), limit).astype(kind)


def setup_inputs(seed: int = 0) -> dict:
    streams_of = jax.random.split(jax.random.key(seed), 12)
    return {
        "conv_input": scatter_about(streams_of[0], (BATCH, SEQ_LEN, CHANNELS), 1.0, 6.0, ((0, 4), (1, 8))),
        "gate_input": scatter_about(streams_of[1], (BATCH, SEQ_LEN, INNER), 1.0, 6.0, ((0, 4), (1, 8))),
        "step_input": draw_step_input(jax.random.fold_in(streams_of[11], 71), 0),
        "filter_taps": scatter_about(streams_of[3], (KERNEL, CHANNELS), KERNEL ** -0.5, 3.0, (), jnp.float32),
        "filter_bias": jnp.clip(jax.random.uniform(streams_of[4], (CHANNELS,), jnp.float32, -0.5, 0.5), -0.5, 0.5),
        "step_bias": jnp.clip(jax.random.uniform(streams_of[5], (HEADS,), jnp.float32, -1.0, 1.0), -1.0, 1.0),
        "decay_log": draw_decay_log(jax.random.fold_in(streams_of[11], 71), 0),
        "skip_gain": jnp.clip(jax.random.uniform(streams_of[7], (HEADS,), jnp.float32, 0.5, 1.5), 0.5, 1.5),
        "norm_weight": jnp.clip(1.0 + 0.1 * jax.random.normal(streams_of[8], (INNER,), jnp.float32), 0.5, 1.5),
        "output_weight": scatter_about(streams_of[9], (INNER, WIDTH), INNER ** -0.5, 0.125, ((0, 4),)),
        "output_grad": scatter_about(streams_of[10], (BATCH, SEQ_LEN, WIDTH), 1.0, 6.0, ((0, 4), (1, 8))),
    }


HIGHEST = lax.Precision.HIGHEST
MASKED = -1e+30
EPSILON = 1e-05

def block_step(skip_gain, carried, slices):
    activated, block_steps, block_rates = slices
    length = activated.shape[0]
    values = activated[:, :INNER].reshape(length, HEADS, HEAD_DIM)
    key_side = activated[:, INNER:INNER + STATE]
    query_side = activated[:, INNER + STATE:]
    cumsums = jnp.cumsum(block_rates, axis=1)
    scaled = values * block_steps.T[:, :, None]
    to_end = jnp.exp(cumsums[:, -1:] - cumsums)
    block_state = jnp.einsum('hs,shp,sn->hpn', to_end, scaled, key_side, precision=HIGHEST)
    scores = jnp.einsum('tn,sn->ts', query_side, key_side, precision=HIGHEST)
    differences = cumsums[:, :, None] - cumsums[:, None, :]
    causal = jnp.tril(jnp.ones((length, length), dtype=bool))
    weights = scores[None] * jnp.exp(jnp.where(causal[None], differences, MASKED))
    inside = jnp.einsum('hts,shp->thp', weights, scaled, precision=HIGHEST)
    from_state = jnp.einsum('tn,hpn->thp', query_side, carried, precision=HIGHEST) * jnp.exp(cumsums).T[:, :, None]
    result = inside + from_state + skip_gain[:, None] * values
    updated = jnp.exp(cumsums[:, -1])[:, None, None] * carried + block_state
    return (updated, result.reshape(length, INNER))

def layer_forward(raw_rows, gate_rows, step_rows, filter_taps, filter_bias, step_bias, decay_log, skip_gain, norm_weight):
    length = raw_rows.shape[0]
    padded = jnp.concatenate([jnp.zeros((KERNEL - 1, CHANNELS), jnp.float32), raw_rows], axis=0)
    filtered = filter_bias + filter_taps[0] * padded[0:length]
    for offset in range(1, KERNEL):
        filtered = filtered + filter_taps[offset] * padded[offset:offset + length]
    activated = jax.nn.silu(filtered)
    step_sizes = jax.nn.softplus(step_rows + step_bias[:, None])
    decay_rates = step_sizes * (-jnp.exp(decay_log))[:, None]
    blocks = length // SPAN
    pieces = (activated.reshape(blocks, SPAN, CHANNELS), step_sizes.reshape(HEADS, blocks, SPAN).transpose(1, 0, 2), decay_rates.reshape(HEADS, blocks, SPAN).transpose(1, 0, 2))
    stepper = jax.checkpoint(lambda carried, slices: block_step(skip_gain, carried, slices))
    _, outputs = lax.scan(stepper, jnp.zeros((HEADS, HEAD_DIM, STATE), jnp.float32), pieces)
    scanned = outputs.reshape(length, INNER)
    gated = scanned * jax.nn.silu(gate_rows)
    inverse_rms = lax.rsqrt(lax.optimization_barrier(jnp.mean(gated * gated, axis=1, keepdims=True)) + EPSILON)
    return gated * inverse_rms * norm_weight

def reference(conv_input, gate_input, step_input, filter_taps, filter_bias, step_bias, decay_log, skip_gain, norm_weight, output_weight, output_grad):

    def one_sequence(slices):
        raw_rows, gate_rows, step_rows, cotangent = slices
        normed, pullback = jax.vjp(layer_forward, raw_rows.astype(jnp.float32), gate_rows.astype(jnp.float32), step_rows, filter_taps, filter_bias, step_bias, decay_log, skip_gain, norm_weight)
        normed_low = normed.astype(jnp.bfloat16)
        normed_grad = jnp.dot(cotangent, output_weight.T, preferred_element_type=jnp.float32)
        weight_term = jnp.dot(normed_low.T, cotangent, preferred_element_type=jnp.float32)
        return tuple(pullback(normed_grad)) + (weight_term,)
    results = lax.map(one_sequence, (conv_input, gate_input, step_input, output_grad))
    input_grad = results[0].astype(jnp.bfloat16)
    gate_grad = results[1].astype(jnp.bfloat16)
    step_grad = results[2]
    filter_grads = jnp.concatenate([lax.optimization_barrier(jnp.sum(results[3], axis=0)), lax.optimization_barrier(jnp.sum(results[4], axis=0))[None]], axis=0)
    head_grads = jnp.stack([lax.optimization_barrier(jnp.sum(results[5], axis=0)), lax.optimization_barrier(jnp.sum(results[6], axis=0)), lax.optimization_barrier(jnp.sum(results[7], axis=0))])
    norm_grad = lax.optimization_barrier(jnp.sum(results[8], axis=0))
    weight_grad = lax.optimization_barrier(jnp.sum(results[9], axis=0))
    return (input_grad, gate_grad, step_grad, weight_grad, filter_grads, norm_grad, head_grads)
```

```python
import jax
import jax.numpy as jnp
from jax import lax
from jax.sharding import PartitionSpec as P

HEADS = 40
HEAD_DIM = 64
STATE = 128
SPAN = 256
INNER = 2560


PRECISE = lax.Precision.HIGH
MASKED = -1e30
EPSILON = 1e-05


def passed_along(value, axis, steps):
    count = lax.axis_size(axis)
    first, last = (max(0, -steps), min(count, count - steps))
    return lax.ppermute(value, axis, [(source, source + steps) for source in range(first, last)])


def spread(table, axis):
    count = lax.axis_size(axis)
    return lax.all_to_all(
        jnp.broadcast_to(table[None], (count,) + table.shape),
        axis,
        split_axis=0,
        concat_axis=0,
        tiled=True,
    )


def carried(states, decay_table, axis, reverse):
    count = lax.axis_size(axis)
    heads, features, width = states.shape
    pieces = states.reshape(heads, count, features // count, width).transpose(1, 0, 2, 3)
    pieces = lax.all_to_all(pieces, axis, split_axis=0, concat_axis=0, tiled=True)
    running = jnp.zeros(pieces.shape[1:], jnp.float32)
    found = [None] * count
    for at in reversed(range(count)) if reverse else range(count):
        found[at] = running
        running = decay_table[at][:, None, None] * running + pieces[at]
    back = lax.all_to_all(jnp.stack(found), axis, split_axis=0, concat_axis=0, tiled=True)
    return back.transpose(1, 0, 2, 3).reshape(heads, features, width)


def summed_everywhere(parts, axes):
    count = 1
    for axis in axes:
        count = count * lax.axis_size(axis)
    flat = jnp.concatenate([part.reshape(-1) for part in parts])
    chunk = -(-flat.shape[0] // (count * 128)) * 128
    padded = jnp.pad(flat, (0, chunk * count - flat.shape[0])).reshape(count, chunk)
    terms = lax.all_to_all(padded, axes, split_axis=0, concat_axis=0, tiled=True)
    total = lax.all_gather(jnp.sum(terms, axis=0), axes, axis=0, tiled=True)
    results, start = [], 0
    for part in parts:
        results.append(total[start : start + part.size].reshape(part.shape))
        start += part.size
    return results


def prepare(extended, step_rows, filter_taps, filter_bias, step_bias, decay_log):
    width = filter_taps.shape[0]
    length = extended.shape[0] - width + 1
    filtered = filter_bias + filter_taps[0] * extended[0:length]
    for offset in range(1, width):
        filtered = filtered + filter_taps[offset] * extended[offset : offset + length]
    activated = jax.nn.silu(filtered)
    step_sizes = jax.nn.softplus(step_rows + step_bias[:, None])
    decay_rates = step_sizes * (-jnp.exp(decay_log))[:, None]
    blocks = length // SPAN
    cumsums = jnp.cumsum(decay_rates.reshape(HEADS, blocks, SPAN), axis=2)
    values = activated[:, :INNER].reshape(blocks, SPAN, HEADS, HEAD_DIM)
    key_side = activated[:, INNER : INNER + STATE].reshape(blocks, SPAN, STATE)
    scaled = values * step_sizes.reshape(HEADS, blocks, SPAN).transpose(1, 2, 0)[..., None]
    to_end = jnp.exp(cumsums[:, :, -1:] - cumsums)
    block_states = jnp.einsum("hcs,cshp,csn->chpn", to_end, scaled, key_side, precision=PRECISE)
    decays = jnp.exp(cumsums[:, :, -1]).T
    return (activated, cumsums, scaled, block_states, decays)


def finish(
    activated, cumsums, scaled, block_states, decays, entering, skip_gain, gate_rows, norm_weight
):
    blocks = cumsums.shape[1]
    length = blocks * SPAN
    values = activated[:, :INNER].reshape(blocks, SPAN, HEADS, HEAD_DIM)
    key_side = activated[:, INNER : INNER + STATE].reshape(blocks, SPAN, STATE)
    query_side = activated[:, INNER + STATE :].reshape(blocks, SPAN, STATE)
    starting = []
    starting.append(entering)
    starting = jnp.stack(starting)
    scores = jnp.einsum("ctn,csn->cts", query_side, key_side, precision=PRECISE)
    differences = cumsums[:, :, :, None] - cumsums[:, :, None, :]
    causal = jnp.tril(jnp.ones((SPAN, SPAN), dtype=bool))
    weights = scores[None] * jnp.exp(jnp.where(causal, differences, MASKED))
    inside = jnp.einsum("hcts,cshp->cthp", weights, scaled, precision=PRECISE)
    from_state = (
        jnp.einsum("ctn,chpn->cthp", query_side, starting, precision=PRECISE)
        * jnp.exp(cumsums).transpose(1, 2, 0)[..., None]
    )
    result = inside + from_state + skip_gain[:, None] * values
    scanned = result.reshape(length, INNER)
    gated = scanned * jax.nn.silu(gate_rows)
    inverse_rms = lax.rsqrt(jnp.mean(gated * gated, axis=1, keepdims=True) + EPSILON)
    return gated * inverse_rms * norm_weight


def body(
    conv_input,
    gate_input,
    step_input,
    filter_taps,
    filter_bias,
    step_bias,
    decay_log,
    skip_gain,
    norm_weight,
    output_weight,
    output_grad,
):
    kernel_rows = filter_taps.shape[0] - 1
    raw_rows = conv_input[0]
    before = passed_along(raw_rows[-kernel_rows:], "seq", 1)
    extended = jnp.concatenate([before, raw_rows], axis=0).astype(jnp.float32)
    gate_rows = gate_input[0].astype(jnp.float32)
    step_rows = step_input[0]
    cotangent = output_grad[0]
    tokens = cotangent.shape[0]
    primals, pull_first = jax.vjp(
        prepare, extended, step_rows, filter_taps, filter_bias, step_bias, decay_log
    )
    activated, cumsums, scaled, block_states, decays = primals
    decay_table = spread(decays[0], "seq")
    entering = carried(block_states[0], decay_table, "seq", False)
    normed, pull_second = jax.vjp(
        finish,
        activated,
        cumsums,
        scaled,
        block_states,
        decays,
        entering,
        skip_gain,
        gate_rows,
        norm_weight,
    )
    normed_low = normed.astype(jnp.bfloat16)
    groups = lax.axis_size("dp")
    own_rows = output_weight.shape[0]
    everyone = lax.all_gather(cotangent, "dp", axis=0, tiled=True)
    partial_columns = lax.dot_general(
        everyone, output_weight, (((1,), (1,)), ((), ())), preferred_element_type=jnp.float32
    )
    regrouped = partial_columns.reshape(groups, tokens, own_rows)
    normed_grad = lax.all_to_all(regrouped, "dp", split_axis=0, concat_axis=2, tiled=True).reshape(
        tokens, groups * own_rows
    )
    own_columns = lax.all_to_all(normed_low, "dp", split_axis=1, concat_axis=0, tiled=True)
    weight_piece = lax.dot_general(
        own_columns, everyone, (((0,), (0,)), ((), ())), preferred_element_type=jnp.float32
    )
    spans = lax.axis_size("seq")
    weight_terms = lax.all_to_all(
        weight_piece.astype(jnp.bfloat16).reshape(spans, own_rows // spans, -1),
        "seq",
        split_axis=0,
        concat_axis=0,
        tiled=True,
    )
    weight_rows = jnp.sum(weight_terms.astype(jnp.float32), axis=0)
    weight_grad = lax.all_gather(weight_rows, "seq", axis=0, tiled=True)
    second = pull_second(normed_grad)
    (
        grad_activated,
        grad_cumsums,
        grad_scaled,
        grad_states,
        grad_decays,
        grad_entering,
        grad_skip,
        grad_gate,
        grad_norm,
    ) = second
    end_grad = carried(grad_entering, decay_table, "seq", True)
    decay_grad = jnp.sum(end_grad * entering, axis=(1, 2))
    first = pull_first(
        (
            grad_activated,
            grad_cumsums,
            grad_scaled,
            grad_states + end_grad[None],
            grad_decays + decay_grad[None],
        )
    )
    grad_extended, grad_steps, grad_taps, grad_bias, grad_step_bias, grad_decay_log = first
    returned = passed_along(grad_extended[:kernel_rows], "seq", -1)
    own_part = grad_extended[kernel_rows:]
    own_part = jnp.concatenate(
        [own_part[:-kernel_rows], own_part[-kernel_rows:] + returned], axis=0
    )
    filter_part = jnp.concatenate([grad_taps, grad_bias[None]], axis=0)
    head_part = jnp.stack([grad_step_bias, grad_decay_log, grad_skip])
    filter_grads, norm_grad, head_grads = summed_everywhere(
        (filter_part, grad_norm, head_part), ("seq", "dp")
    )
    input_grad = own_part.astype(jnp.bfloat16)[None]
    gate_grad = grad_gate.astype(jnp.bfloat16)[None]
    step_grad = grad_steps[None]
    return (input_grad, gate_grad, step_grad, weight_grad, filter_grads, norm_grad, head_grads)


def solution(mesh):
    return jax.shard_map(
        body,
        mesh=mesh,
        in_specs=(
            P("dp", "seq", None),
            P("dp", "seq", None),
            P("dp", None, "seq"),
            P(),
            P(),
            P(),
            P(),
            P(),
            P(),
            P("dp", None),
            P("dp", "seq", None),
        ),
        out_specs=(
            P("dp", "seq", None),
            P("dp", "seq", None),
            P("dp", None, "seq"),
            P("dp", None),
            P(),
            P(),
            P(),
        ),
        check_vma=False,
    )
```
